32 devices in a mesh: grp: 8 (over z, x), loc: 4 (over y, core).
Axes of the slice: x: 2, y: 2, z: 4, core: 2. Of those that a mesh axis runs over, the one named last changes fastest.
Arguments:
- features: bfloat16 [32768, 2048], P(('grp', 'loc')), may hold values from -6 to 6
- weight: bfloat16 [2048, 2048], replicated, may hold values from -0.125 to 0.125
- bias: float32 [2048], replicated, may hold values from -2.5 to 2.5
- cotangent: bfloat16 [32768, 2048], P(('grp', 'loc')), may hold values from -6 to 6
- neighbours: int32 [32768, 64], P(('grp', 'loc')), may hold values from 0 to 127, as said below
- edge_mask: int32 [32768, 64], P(('grp', 'loc')), may hold values from 0 to 1, as said below
- cluster_ids: int32 [32768], P(('grp', 'loc')), may hold values from 0 to 127, as said below
- row_mask: int32 [32768], P(('grp', 'loc')), may hold values from 0 to 1
Outputs:
- activations: bfloat16 [32768, 2048], P(('grp', 'loc'))
- grad_features: bfloat16 [32768, 2048], P(('grp', 'loc'))
- grad_weight: float32 [2048, 2048], replicated
- grad_bias: float32 [2048], replicated
The draws below stay inside these ranges and needn't reach their ends.
Inputs may be any that keep to these rules, and one draw needn't show every extreme that they name: `neighbours`: positions within the node's own tile of 128 slots. `edge_mask`: each row's live entries come first. `cluster_ids`: starts at 0 in every tile, never falls within a tile and rises by at most one from slot to slot.
All inputs are finite; a program needn't handle non-finite values.
Results may differ from the reference program's by a relative error of at most 0.009.
The reference program's roundings to bfloat16 on the way count: a program that leaves them out, or rounds other values in their place, can miss the bound.
Values sent between devices are 32-bit elements; how exact they have to be, the bound alone decides.
No kernel may reach another device: no remote copies, remote signals or barrier semaphores. Data moves between devices by JAX's collectives and lax.ppermute only.
A program may use at most 128 MiB of HBM per device.

```python
import jax
import jax.numpy as jnp
from jax import lax

D = 2048
TILE = 128
NBRS = 64
NODES = 32768


def draw_neighbours(key, part):
    position = jnp.arange(NODES, dtype=jnp.int32) % TILE
    offset = jax.random.randint(key, (NODES, NBRS), -12, 13, dtype=jnp.int32)
    return ((position[:, None] + offset) % TILE).astype(jnp.int32)


def draw_edge_mask(key, part):
    live_count = jax.random.randint(key, (NODES, 1), 16, NBRS + 1, dtype=jnp.int32)
    return (jnp.arange(NBRS, dtype=jnp.int32)[None, :] < live_count).astype(jnp.int32)


def draw_cluster_ids(key, part):
    slot = jnp.arange(NODES, dtype=jnp.int32)
    position = slot % TILE
    starts = (jax.random.randint(key, (NODES,), 0, 8, dtype=jnp.int32) == 0).astype(jnp.int32)
    last_tile = (slot >= NODES - TILE).astype(jnp.int32)
    starts = jnp.maximum(starts, last_tile)
    starts = starts * (position != 0).astype(jnp.int32)
    return jnp.cumsum(starts.reshape(NODES // TILE, TILE), axis=1).reshape(NODES).astype(jnp.int32)


def draw_row_mask(key, part):
    return (jax.random.randint(key, (NODES,), 0, 8, dtype=jnp.int32) != 0).astype(jnp.int32)


def draw_bias(key, part):
    sign_key = jax.random.fold_in(key, 11)
    size_key = jax.random.fold_in(key, 12)
    sign = jnp.where(jax.random.uniform(sign_key, (D,), jnp.float32) < 0.5, -1.0, 1.0)
    magnitude = jax.random.uniform(size_key, (D,), jnp.float32, 1.0, 2.5)
    return (sign * magnitude).astype(jnp.float32)


def raised(values, rng, source, target, shards_of, factor):
    owner, partner = [(jnp.arange(values.shape[axis_at]) // (values.shape[axis_at] // shards_of)).reshape([-1 if axis == axis_at else 1 for axis in range(values.ndim)]) for axis_at in (source, target)]
    chosen = jax.random.permutation(rng, shards_of)[partner]
    strong = (owner == chosen) | (owner == (partner + shards_of // 2) % shards_of)
    return jnp.where(strong, factor * values, values)


def steps_of(own_key, shape, shards, low, top_value):
    level, own = 1.0, jax.random.fold_in(own_key, 6)
    for dim, parts in shards:
        steps = jnp.exp(jax.random.uniform(jax.random.fold_in(own, dim), (parts,), jnp.float32, low / len(shards), top_value / len(shards)))
        level = level * jnp.repeat(steps, shape[dim] // parts).reshape([-1 if axis == dim else 1 for axis in range(len(shape))])
    return level


def scatter_about(own_key, extent, deviation, limit, shards=(), kind=jnp.bfloat16):
    loudness = steps_of(own_key, extent, shards, -0.22, 0.18) if shards else 1.0
    entries = jax.random.normal(own_key, extent, jnp.float32) * deviation * loudness
    return jnp.minimum(jnp.maximum(entries, -limit), limit).astype(kind)


def heavy_noise(stream_key, shape, deviation, reach, cuts, heavy, kind=jnp.bfloat16):
    values = deviation * jax.random.normal(stream_key, shape, jnp.float32)
    if cuts:
        values = values * steps_of(stream_key, shape, cuts, -0.22, 0.18)
    return jnp.clip(raised(values, jax.random.fold_in(stream_key, 3), *heavy), -reach, reach).astype(kind)


def setup_inputs(seed: int = 0) -> dict:
    seeds = jax.random.split(jax.random.key(seed), 9)
    return {
        "features": heavy_noise(seeds[0], (NODES, D), 1.0, 6.0, ((0, 32),), (0, 1, 32, 2.75)),
        "weight": scatter_about(seeds[1], (D, D), D ** -0.5, 0.125),
        "bias": draw_bias(jax.random.fold_in(seeds[8], 71), 0),
        "cotangent": scatter_about(seeds[3], (NODES, D), 1.0, 6.0, ((0, 32),)),
        "neighbours": draw_neighbours(jax.random.fold_in(seeds[8], 71), 0),
        "edge_mask": draw_edge_mask(jax.random.fold_in(seeds[8], 71), 0),
        "cluster_ids": draw_cluster_ids(jax.random.fold_in(seeds[8], 71), 0),
        "row_mask": draw_row_mask(jax.random.fold_in(seeds[8], 71), 0),
    }


@jax.custom_vjp
def low(v):
    return lax.optimization_barrier(v.astype(jnp.bfloat16)).astype(jnp.float32)

@jax.custom_vjp
def low_back(v):
    return v

def low_keep(v):
    return (low(v), None)

def low_pass(kept, grad):
    return (grad,)

def back_keep(v):
    return (v, None)

def back_low(kept, grad):
    return (low(grad),)
low.defvjp(low_keep, low_pass)
low_back.defvjp(back_keep, back_low)

def build_tile(near, live_edges, clusters, present):
    width = near.shape[0]
    position = jnp.arange(width, dtype=jnp.int32)
    matched = (near[:, :, None] == position[None, None, :]) & (live_edges[:, :, None] == 1)
    edge_hits = lax.optimization_barrier(jnp.sum(matched.astype(jnp.int32), axis=1))
    allowed = (clusters[:, None] == clusters[None, :]) & (position[:, None] != position[None, :])
    allowed = allowed & (present[:, None] == 1) & (present[None, :] == 1)
    adjacency = jnp.where(allowed, edge_hits, 0).astype(jnp.float32)
    degree = lax.optimization_barrier(jnp.sum(adjacency, axis=1))
    self_loops = jnp.where((position[:, None] == position[None, :]) & (present[:, None] == 1), 2.0, 0.0).astype(jnp.float32)
    return (adjacency + self_loops) / (degree + 1.0)[:, None]

def reference(features, weight, bias, cotangent, neighbours, edge_mask, cluster_ids, row_mask):
    tile_count = NODES // TILE
    pieces = (neighbours.reshape(tile_count, TILE, NBRS), edge_mask.reshape(tile_count, TILE, NBRS), cluster_ids.reshape(tile_count, TILE), row_mask.reshape(tile_count, TILE))
    propagator = low(lax.map(lambda group: build_tile(*group), pieces))

    def forward(hidden_in, weight_in, bias_in):
        aggregated = jnp.einsum('tij,tjd->tid', propagator, hidden_in.reshape(tile_count, TILE, D), precision=lax.Precision.HIGHEST).reshape(NODES, D)
        agg_low = low(low_back(aggregated))
        pre = low_back(jnp.dot(agg_low, weight_in, precision=lax.Precision.HIGHEST) + bias_in)
        return jax.nn.relu(pre)
    result, pullback = jax.vjp(forward, features.astype(jnp.float32), weight.astype(jnp.float32), bias.astype(jnp.float32))
    grad_in, grad_w, grad_b = pullback(cotangent.astype(jnp.float32))
    return (result.astype(jnp.bfloat16), grad_in.astype(jnp.bfloat16), grad_w, grad_b)
```

```python
import functools

import jax
import jax.numpy as jnp
from jax import lax
from jax.experimental import pallas as pl
from jax.experimental.pallas import tpu as pltpu
from jax.sharding import PartitionSpec as P

TILE = 128
BF16 = jnp.bfloat16
F32 = jnp.float32

GROUPS = ((2, "xyz"), (2, "zxy"), (2, "xyz"), (2, "xyz"))
ORDER = (
    "g0", "g1", "r00", "r10", "g2", "r01", "r20", "r02", "g3", "r11", "r21", "r03", "r30", "r12", "r22", "a00",
    "r23", "r31", "a01", "r13", "r32", "a20", "a02", "r33", "a10", "a21", "c0", "w00", "a11", "a30", "w01",
    "a22", "a31", "a12", "f0", "f1", "c2", "f2", "w21", "a32", "f3", "c1", "w10", "w11", "w20", "c3", "w30",
    "w31",
)

COST = pl.CostEstimate(flops=25 * 10**9, bytes_accessed=2**20, transcendentals=0)
DONE = jax.ShapeDtypeStruct((8, 128), F32)
VMEM = pl.BlockSpec(memory_space=pltpu.VMEM)
ANY = pl.BlockSpec(memory_space=pl.ANY)


def tile_kernel(near_ref, live_ref, cluster_ref, present_ref, features_ref, prop_ref, mixed_ref):
    tiles = cluster_ref.shape[0]
    step = pl.program_id(0)
    slot = lax.broadcasted_iota(jnp.int32, (TILE, TILE), 0)
    node = lax.broadcasted_iota(jnp.int32, (TILE, TILE), 1)
    slot_low = slot.astype(F32).astype(BF16)
    one, zero = jnp.ones((TILE, TILE), BF16), jnp.zeros((TILE, TILE), BF16)
    for t in range(tiles):
        part = slice(t * TILE, (t + 1) * TILE)
        near = jnp.where(live_ref[:, part] == 1, near_ref[:, part], -1).astype(F32).astype(BF16)
        hits = zero
        for k in range(near.shape[0]):
            hits = hits + jnp.where(near[k : k + 1, :] == slot_low, one, zero)
        key = jnp.where(present_ref[t] == 1, cluster_ref[t], -1).astype(F32)
        along = jnp.broadcast_to(key, (TILE, TILE))
        down = along.T
        allowed = (along == down) & (along >= 0.0) & (slot != node)
        adjacency = jnp.where(allowed, hits.astype(F32), 0.0)
        degree = jnp.sum(adjacency, axis=0, keepdims=True)
        self_loops = jnp.where((slot == node) & (along >= 0.0), 2.0, 0.0)
        prop_t = (adjacency + self_loops) / (degree + 1.0)
        at = step * tiles + t
        prop_ref[at] = prop_t.astype(BF16)
        prop = prop_t.T.astype(BF16)
        mixed = jnp.dot(prop, features_ref[part, :], preferred_element_type=F32)
        mixed_ref[pl.ds(pl.multiple_of(at * TILE, TILE), TILE), :] = mixed.astype(BF16)


def propagate(features, neighbours, edge_mask, cluster_ids, row_mask):
    rows, width = features.shape
    tiles = rows // TILE
    nbrs = neighbours.shape[1]
    each = 2
    block = each * TILE
    inputs = (
        neighbours.T,
        edge_mask.T,
        cluster_ids.reshape(tiles, 1, TILE),
        row_mask.reshape(tiles, 1, TILE),
        features,
    )
    return pl.pallas_call(
        tile_kernel,
        grid=(tiles // each,),
        in_specs=[
            pl.BlockSpec((nbrs, block), lambda t: (0, t)),
            pl.BlockSpec((nbrs, block), lambda t: (0, t)),
            pl.BlockSpec((each, 1, TILE), lambda t: (t, 0, 0)),
            pl.BlockSpec((each, 1, TILE), lambda t: (t, 0, 0)),
            pl.BlockSpec((block, width), lambda t: (t, 0)),
        ],
        out_specs=[VMEM, VMEM],
        out_shape=[
            jax.ShapeDtypeStruct((tiles, TILE, TILE), BF16),
            jax.ShapeDtypeStruct((rows, width), BF16),
        ],
        compiler_params=pltpu.CompilerParams(vmem_limit_bytes=12 * 2**20),
        cost_estimate=pl.CostEstimate(
            flops=2 * rows * width * width // 2, bytes_accessed=2 * rows * width, transcendentals=0
        ),
        name="propagate",
    )(*(pltpu.with_memory_space_constraint(v, pltpu.HBM) for v in inputs))


def layer_kernel(start, line, base_ref, mixed_ref, weight_ref, bias_ref, cot_ref, token_ref, *rest):
    act_out, gp_ref, theirs_ref, mine_ref, act_ref, cot_in, act_sem, cot_sem = rest[-8:]
    rows, cols = act_ref.shape
    block = min(rows, 512)
    half = (mine_ref.shape[0] - 8) // 2
    chunk = half // 4
    here = slice(start, start + cols)
    load = pltpu.make_async_copy(cot_ref.at[:, pl.ds(start, cols)], cot_in, cot_sem)
    load.start()
    total = jnp.zeros((1, cols), F32)
    for i in range(rows // block):
        part = slice(i * block, (i + 1) * block)
        pre = jnp.dot(mixed_ref[part, :], weight_ref[:, here], preferred_element_type=F32) + bias_ref[:, here]
        act_ref[part, :] = jnp.maximum(pre, 0.0).astype(BF16)
        if i == 0:
            load.wait()
        grad = jnp.where(pre > 0.0, cot_in[part, :].astype(F32), 0.0).astype(BF16)
        gp_ref[part, here] = grad
        total = total + jnp.sum(grad.astype(F32), axis=0, keepdims=True)
    store = pltpu.make_async_copy(act_ref, act_out.at[:, pl.ds(start, cols)], act_sem)
    store.start()

    for side, out_ref in ((0, theirs_ref), (1, mine_ref)):
        for j in range(2):
            from_row = pl.multiple_of((base_ref[line + side] // 8) * 2 * half + j * half, half)
            share = lax.dot_general(
                mixed_ref[:, pl.ds(from_row, half)],
                gp_ref[:, here],
                (((0,), (0,)), ((), ())),
                preferred_element_type=F32,
            )
            for m in range(4):
                spot = ((j * 4 + m) ^ (base_ref[line + side] % 8)) * chunk
                out_ref[pl.ds(pl.multiple_of(spot, chunk), chunk), :] = share[m * chunk : (m + 1) * chunk]
        out_ref[2 * half :, :] = jnp.broadcast_to(total, (8, cols))
    store.wait()


def layer_group(name, base, line, mixed, weight, bias, cotangent, token, carried, start, cols):
    rows, width = mixed.shape
    share = jax.ShapeDtypeStruct((width // 2 + 8, cols), F32)
    return pl.pallas_call(
        functools.partial(layer_kernel, start, line),
        grid_spec=pltpu.PrefetchScalarGridSpec(
            num_scalar_prefetch=1,
            grid=(1,),
            in_specs=[VMEM, VMEM, VMEM, ANY, ANY] + ([ANY, VMEM] if carried else []),
            out_specs=[ANY, VMEM, VMEM, VMEM],
            scratch_shapes=[
                pltpu.VMEM((rows, cols), BF16),
                pltpu.VMEM((rows, cols), BF16),
                pltpu.SemaphoreType.DMA,
                pltpu.SemaphoreType.DMA,
            ],
        ),
        out_shape=[
            jax.ShapeDtypeStruct((rows, width), BF16),
            jax.ShapeDtypeStruct((rows, width), BF16),
            share,
            share,
        ],
        input_output_aliases={6: 0, 7: 1} if carried else {},
        compiler_params=pltpu.CompilerParams(vmem_limit_bytes=10 * 2**20),
        cost_estimate=COST,
        name=name,
    )(base, mixed, weight, bias.reshape(1, width), pltpu.with_memory_space_constraint(cotangent, pltpu.HBM), token, *carried)


def join_kernel(plan, *refs):
    outs = refs[len(refs) - len(plan) :]
    for out_ref, pieces in zip(outs, plan):
        at = 0
        for count, terms in pieces:
            value = refs[terms[0][0]][terms[0][1] : terms[0][1] + count, :]
            for index, row in terms[1:]:
                value = value + refs[index][row : row + count, :]
            out_ref[at : at + count, :] = value
            at += count


def join(name, arrays, token, *plan):
    cols = arrays[0].shape[1]
    return pl.pallas_call(
        functools.partial(join_kernel, plan),
        in_specs=[VMEM] * len(arrays) + [ANY],
        out_specs=[VMEM] * len(plan),
        out_shape=[jax.ShapeDtypeStruct((sum(n for n, _ in pieces), cols), F32) for pieces in plan],
        compiler_params=pltpu.CompilerParams(vmem_limit_bytes=12 * 2**20),
        cost_estimate=COST,
        name=name,
    )(*arrays, token)


def place_kernel(side, at, base_ref, first_ref, second_ref, token_ref, *rest):
    out_ref, done_ref, sem = rest[-3:]
    cols = first_ref.shape[1]
    chunk = first_ref.shape[0] // 4
    copies = []
    for r in range(8):
        source = first_ref if r < 4 else second_ref
        spot = pl.multiple_of((base_ref[side] ^ r) * chunk, chunk)
        copies.append(
            pltpu.make_async_copy(
                source.at[pl.ds((r % 4) * chunk, chunk), :],
                out_ref.at[pl.ds(spot, chunk), pl.ds(at, cols)],
                sem.at[r],
            )
        )
    for copy in copies:
        copy.start()
    done_ref[...] = jnp.zeros_like(done_ref)
    for copy in copies:
        copy.wait()


def place(name, base, side, first, second, token, out, width, at):
    carried = [] if out is None else [out]
    return pl.pallas_call(
        functools.partial(place_kernel, side, at),
        grid_spec=pltpu.PrefetchScalarGridSpec(
            num_scalar_prefetch=1,
            grid=(1,),
            in_specs=[VMEM, VMEM, ANY] + [ANY] * len(carried),
            out_specs=[ANY, VMEM],
            scratch_shapes=[pltpu.SemaphoreType.DMA((8,))],
        ),
        out_shape=[jax.ShapeDtypeStruct((width, width), F32), DONE],
        input_output_aliases={4: 0} if carried else {},
        compiler_params=pltpu.CompilerParams(vmem_limit_bytes=12 * 2**20),
        cost_estimate=COST,
        name=name,
    )(base, first, second, token, *carried)


def back_kernel(index, gp_ref, weight_ref, prop_ref, token_ref, *rest):
    out_ref, done_ref = rest[-2:]
    done_ref[...] = jnp.zeros_like(done_ref)
    part, cols = out_ref.shape
    j = pl.program_id(0)
    cut = pl.ds(pl.multiple_of(j * cols, cols), cols)
    mixed = lax.dot_general(
        gp_ref[index * part : (index + 1) * part, :],
        weight_ref[cut, :],
        (((1,), (1,)), ((), ())),
        preferred_element_type=F32,
    ).astype(BF16)
    for t in range(part // TILE):
        rows = slice(t * TILE, (t + 1) * TILE)
        tile = index * (part // TILE) + t
        out_ref[rows, :] = jnp.dot(prop_ref[tile], mixed[rows], preferred_element_type=F32).astype(BF16)


def back(name, gp, weight, prop_t, token, carried, index, count):
    rows, width = gp.shape
    part = rows // count
    cols = min(width, 512)
    extra = [] if carried is None else [carried]
    return pl.pallas_call(
        functools.partial(back_kernel, index),
        grid=(width // cols,),
        in_specs=[VMEM, VMEM, VMEM, ANY] + [ANY] * len(extra),
        out_specs=[pl.BlockSpec((part, cols), lambda j: (index, j)), VMEM],
        out_shape=[jax.ShapeDtypeStruct((rows, width), BF16), DONE],
        input_output_aliases={4: 0} if extra else {},
        compiler_params=pltpu.CompilerParams(vmem_limit_bytes=16 * 2**20),
        cost_estimate=COST,
        name=name,
    )(gp, weight, prop_t, token, *extra)


def bit_length(n):
    return n.bit_length() - 1


def per_device(groups, locs, features, weight, bias, cotangent, neighbours, edge_mask, cluster_ids, row_mask):
    width = features.shape[1]
    devices = groups * locs
    top, low = bit_length(devices), bit_length(locs)
    y_bits, x_bits, z_bits = list(range(1, low)), list(range(low, top - 2)), [top - 2, top - 1]
    axes = ("grp", "loc")
    number = lax.axis_index("grp") * locs + lax.axis_index("loc")

    def swap(value, pair):
        flip = lambda i: i ^ (1 << pair[i & 1])
        return lax.ppermute(value, axes, [(i, flip(i)) for i in range(devices)])

    core, first, second, near_z = (0, 0), (x_bits[0], y_bits[0]), (y_bits[0], x_bits[0]), (z_bits[0],) * 2
    halving = {"xyz": (first, second, near_z), "zxy": (near_z, first, second)}
    doubling = [(z_bits[1],) * 2] + [(b, b) for b in x_bits[1:] + y_bits[1:]]

    slots, line = [], {}
    for kind in sorted(set(k for _, k in GROUPS)):
        line[kind] = len(slots)
        for side in (1 - number % 2, number % 2):
            spot = side
            for pair in halving[kind]:
                spot = spot * 2 + jnp.where(side == 1, (number >> pair[1]) & 1, (number >> pair[0]) & 1)
            slots.append(spot)
    base = jnp.stack(slots).astype(jnp.int32)

    prop_t, mixed = propagate(features, neighbours, edge_mask, cluster_ids, row_mask)

    count = len(GROUPS)
    unit = width // sum(u for u, _ in GROUPS)
    starts, sizes, kinds = [], [], []
    for u, kind in GROUPS:
        starts.append(sum(sizes))
        sizes.append(u * unit)
        kinds.append(kind)
    fills = sum(e[0] == "f" for e in ORDER)

    terms = [None] * count
    got = [None] * count
    shares = [None] * count
    carried = []
    out = None
    grad_features = None
    token = prop_t
    end = width // 16

    for event in ORDER:
        what, g = event[0], int(event[1])
        stage = int(event[2]) if len(event) > 2 else 0
        if what == "g":
            act, gp, theirs, mine = layer_group(
                event, base, line[kinds[g]], mixed, weight, bias, cotangent, token, carried, starts[g], sizes[g]
            )
            carried = [act, gp]
            terms[g] = [mine, swap(theirs, core)]
            token = theirs
        elif what == "r" and stage < 3:
            n = (width // 2) >> (stage + 1)
            send, keep = join(
                event,
                terms[g],
                token,
                ((n + 8, ((0, n), (1, n))),),
                ((n, ((0, 0), (1, 0))), (8, ((0, 2 * n), (1, 2 * n)))),
            )
            terms[g] = [keep, swap(send, halving[kinds[g]][stage])]
            token = send
        elif what == "r":
            for pair in doubling:
                (total,) = join(event, terms[g], token, ((end + 8, ((0, 0), (1, 0))),))
                terms[g] = [total, swap(total, pair)]
                token = total
        elif what == "a":
            if stage == 0:
                total, shares[g] = join(
                    event, terms[g], token, ((end, ((0, 0), (1, 0))),), ((8, ((0, end), (1, end))),)
                )
            else:
                n = terms[g][0].shape[0]
                (total,) = join(event, terms[g], token, ((n, ((0, 0),)), (n, ((1, 0),))))
            terms[g] = [total, swap(total, halving[kinds[g]][2 - stage])]
            if stage == 2:
                got[g] = [swap(total, core)]
            token = total
        elif what == "c":
            late, _ = lax.optimization_barrier((terms[g][1], token))
            terms[g][1] = late
            got[g].append(swap(late, core))
        elif what == "w":
            pieces = terms[g] if stage == 0 else got[g]
            out, token = place(event, base, line[kinds[g]] + 1 - stage, *pieces, token, out, width, starts[g])
        else:
            grad_features, token = back(event, carried[1], weight, prop_t, token, grad_features, g, fills)
    grad_bias = jnp.concatenate([s[0] for s in shares])
    return carried[0], grad_features, out, grad_bias


def solution(mesh):
    rows = P(("grp", "loc"), None)
    flat = P(("grp", "loc"))
    in_specs = (rows, P(), P(), rows, rows, rows, flat, flat)
    out_specs = (rows, rows, P(), P())
    return jax.shard_map(
        functools.partial(per_device, mesh.shape["grp"], mesh.shape["loc"]),
        mesh=mesh,
        in_specs=in_specs,
        out_specs=out_specs,
        check_vma=False,
    )
```

```python
import functools

import jax
import jax.numpy as jnp
from jax import lax
from jax.experimental import pallas as pl
from jax.experimental.pallas import tpu as pltpu
from jax.sharding import PartitionSpec as P

TILE = 128
BF16 = jnp.bfloat16
F32 = jnp.float32

GROUPS = ((2, "xyz"), (2, "zxy"), (2, "yxz"), (2, "xyz"))
ORDER = (
    "g0", "g1", "r00", "r10", "g2", "r01", "r20", "g3", "r02", "f0", "r11+c3_", "r03", "r21", "r30", "r12",
    "r22", "r13+R03", "a00", "r31", "r23", "a10", "r32", "a01", "f1", "a20+A10", "a11", "r33", "a02", "f2",
    "a30+A11+A20+C00", "a21", "a12+A02", "f3", "a31+C10", "c0", "a22", "a32+C01", "w01+C20", "w00", "c1",
    "w10+C30", "w11", "c2", "w20", "w21", "c3", "w30", "w31",
)

COST = pl.CostEstimate(flops=25 * 10**9, bytes_accessed=2**20, transcendentals=0)
DONE = jax.ShapeDtypeStruct((8, 128), F32)
VMEM = pl.BlockSpec(memory_space=pltpu.VMEM)
ANY = pl.BlockSpec(memory_space=pl.ANY)


def tile_kernel(near_ref, live_ref, cluster_ref, present_ref, features_ref, base_ref, prop_ref, mixed_ref):
    tiles = cluster_ref.shape[0]
    step = pl.program_id(0)
    slot = lax.broadcasted_iota(jnp.int32, (TILE, TILE), 0)
    node = lax.broadcasted_iota(jnp.int32, (TILE, TILE), 1)
    slot_low = slot.astype(F32).astype(BF16)
    one, zero = jnp.ones((TILE, TILE), BF16), jnp.zeros((TILE, TILE), BF16)
    for t in range(tiles):
        part = slice(t * TILE, (t + 1) * TILE)
        near = jnp.where(live_ref[:, part] == 1, near_ref[:, part], -1).astype(F32).astype(BF16)
        hits = zero
        for k in range(near.shape[0]):
            hits = hits + jnp.where(near[k : k + 1, :] == slot_low, one, zero)
        key = jnp.where(present_ref[t] == 1, cluster_ref[t], -1).astype(F32)
        along = jnp.broadcast_to(key, (TILE, TILE))
        down = along.T
        allowed = (along == down) & (along >= 0.0) & (slot != node)
        adjacency = jnp.where(allowed, hits.astype(F32), 0.0)
        degree = jnp.sum(adjacency, axis=0, keepdims=True)
        self_loops = jnp.where((slot == node) & (along >= 0.0), 2.0, 0.0)
        prop_t = (adjacency + self_loops) / (degree + 1.0)
        at = step * tiles + t
        prop_ref[at] = prop_t.astype(BF16)
        prop = prop_t.T.astype(BF16)
        mixed = jnp.dot(prop, features_ref[part, :], preferred_element_type=F32)
        mixed_ref[pl.ds(pl.multiple_of(at * TILE, TILE), TILE), :] = mixed.astype(BF16)


def propagate(features, neighbours, edge_mask, cluster_ids, row_mask, base):
    rows, width = features.shape
    tiles = rows // TILE
    nbrs = neighbours.shape[1]
    each = 2
    block = each * TILE
    inputs = (
        neighbours.T,
        edge_mask.T,
        cluster_ids.reshape(tiles, 1, TILE),
        row_mask.reshape(tiles, 1, TILE),
        features,
    )
    return pl.pallas_call(
        tile_kernel,
        grid=(tiles // each,),
        in_specs=[
            pl.BlockSpec((nbrs, block), lambda t: (0, t)),
            pl.BlockSpec((nbrs, block), lambda t: (0, t)),
            pl.BlockSpec((each, 1, TILE), lambda t: (t, 0, 0)),
            pl.BlockSpec((each, 1, TILE), lambda t: (t, 0, 0)),
            pl.BlockSpec((block, width), lambda t: (t, 0)),
            ANY,
        ],
        out_specs=[VMEM, VMEM],
        out_shape=[
            jax.ShapeDtypeStruct((tiles, TILE, TILE), BF16),
            jax.ShapeDtypeStruct((rows, width), BF16),
        ],
        compiler_params=pltpu.CompilerParams(vmem_limit_bytes=12 * 2**20),
        cost_estimate=pl.CostEstimate(
            flops=2 * rows * width * width // 2, bytes_accessed=2 * rows * width, transcendentals=0
        ),
        name="propagate",
    )(*(pltpu.with_memory_space_constraint(v, pltpu.HBM) for v in inputs), base)


def layer_kernel(start, line, base_ref, mixed_ref, weight_ref, bias_ref, cot_ref, *rest):
    act_ref, cot_in, act_sem, cot_sem = rest[-4:]
    act_out, gp_ref, theirs_ref, mine_ref = rest[-8:-4]
    rows, cols = act_ref.shape
    block = min(rows, 512)
    half = mixed_ref.shape[1] // 4
    chunk = half // 4
    here = slice(start, start + cols)
    load = pltpu.make_async_copy(cot_ref.at[:, pl.ds(start, cols)], cot_in, cot_sem)
    load.start()
    total = jnp.zeros((1, cols), F32)
    for i in range(rows // block):
        part = slice(i * block, (i + 1) * block)
        pre = jnp.dot(mixed_ref[part, :], weight_ref[:, here], preferred_element_type=F32) + bias_ref[:, here]
        act_ref[part, :] = jnp.maximum(pre, 0.0).astype(BF16)
        if i == 0:
            load.wait()
        grad = jnp.where(pre > 0.0, cot_in[part, :].astype(F32), 0.0).astype(BF16)
        gp_ref[part, here] = grad
        total = total + jnp.sum(grad.astype(F32), axis=0, keepdims=True)
    store = pltpu.make_async_copy(act_ref, act_out.at[:, pl.ds(start, cols)], act_sem)
    store.start()

    def share_of(from_row):
        return lax.dot_general(
            mixed_ref[:, pl.ds(from_row, half)],
            gp_ref[:, here],
            (((0,), (0,)), ((), ())),
            preferred_element_type=F32,
        )

    total = jnp.broadcast_to(total, (8, cols))
    for side, out_ref in ((0, theirs_ref), (1, mine_ref)):
        for j in range(2):
            share = share_of(pl.multiple_of((base_ref[line + side] // 8) * 2 * half + j * half, half))
            for m in range(4):
                spot = ((j * 4 + m) ^ (base_ref[line + side] % 8)) * chunk
                out_ref[pl.ds(pl.multiple_of(spot, chunk), chunk), :] = share[m * chunk : (m + 1) * chunk]
        out_ref[2 * half :, :] = total
    store.wait()


def layer_group(name, base, line, mixed, weight, bias, cotangent, waits, carried, start, cols):
    rows, width = mixed.shape
    share = jax.ShapeDtypeStruct((width // 2 + 8, cols), F32)
    return pl.pallas_call(
        functools.partial(layer_kernel, start, line),
        grid_spec=pltpu.PrefetchScalarGridSpec(
            num_scalar_prefetch=1,
            grid=(1,),
            in_specs=[VMEM, VMEM, VMEM, ANY] + [ANY] * len(waits) + ([ANY, VMEM] if carried else []),
            out_specs=[ANY, VMEM, VMEM, VMEM],
            scratch_shapes=[
                pltpu.VMEM((rows, cols), BF16),
                pltpu.VMEM((rows, cols), BF16),
                pltpu.SemaphoreType.DMA,
                pltpu.SemaphoreType.DMA,
            ],
        ),
        out_shape=[
            jax.ShapeDtypeStruct((rows, width), BF16),
            jax.ShapeDtypeStruct((rows, width), BF16),
            share,
            share,
        ],
        input_output_aliases={5 + len(waits): 0, 6 + len(waits): 1} if carried else {},
        compiler_params=pltpu.CompilerParams(vmem_limit_bytes=10 * 2**20),
        cost_estimate=COST,
        name=name,
    )(
        base,
        mixed,
        weight,
        bias.reshape(1, width),
        pltpu.with_memory_space_constraint(cotangent, pltpu.HBM),
        *waits,
        *carried,
    )


def join_kernel(plan, *refs):
    outs = refs[len(refs) - len(plan) :]
    for out_ref, pieces in zip(outs, plan):
        at = 0
        for count, terms in pieces:
            value = refs[terms[0][0]][terms[0][1] : terms[0][1] + count, :]
            for index, row in terms[1:]:
                value = value + refs[index][row : row + count, :]
            out_ref[at : at + count, :] = value
            at += count


def join(name, arrays, waits, *plan):
    cols = arrays[0].shape[1]
    return pl.pallas_call(
        functools.partial(join_kernel, plan),
        in_specs=[VMEM] * len(arrays) + [ANY] * len(waits),
        out_specs=[VMEM] * len(plan),
        out_shape=[jax.ShapeDtypeStruct((sum(n for n, _ in pieces), cols), F32) for pieces in plan],
        compiler_params=pltpu.CompilerParams(vmem_limit_bytes=12 * 2**20),
        cost_estimate=COST,
        name=name,
    )(*arrays, *waits)


def placing(base_ref, jobs, refs, out_ref, sems):
    copies = []
    for n, (side, at) in enumerate(jobs):
        cols = refs[2 * n].shape[1]
        chunk = refs[2 * n].shape[0] // 4
        for r in range(8):
            spot = pl.multiple_of((base_ref[side] ^ r) * chunk, chunk)
            copies.append(
                pltpu.make_async_copy(
                    refs[2 * n + r // 4].at[pl.ds((r % 4) * chunk, chunk), :],
                    out_ref.at[pl.ds(spot, chunk), pl.ds(at, cols)],
                    sems.at[8 * n + r],
                )
            )
    return copies


def place_kernel(jobs, base_ref, *rest):
    out_ref, done_ref, sems = rest[-3:]
    copies = placing(base_ref, jobs, rest[: 2 * len(jobs)], out_ref, sems)
    for copy in copies:
        copy.start()
    done_ref[...] = jnp.zeros_like(done_ref)
    for copy in copies:
        copy.wait()


def place(name, base, jobs, pieces, waits, out, width):
    carried = [] if out is None else [out]
    return pl.pallas_call(
        functools.partial(place_kernel, jobs),
        grid_spec=pltpu.PrefetchScalarGridSpec(
            num_scalar_prefetch=1,
            grid=(1,),
            in_specs=[VMEM] * len(pieces) + [ANY] * (len(waits) + len(carried)),
            out_specs=[ANY, VMEM],
            scratch_shapes=[pltpu.SemaphoreType.DMA((8 * len(jobs),))],
        ),
        out_shape=[jax.ShapeDtypeStruct((width, width), F32), DONE],
        input_output_aliases={1 + len(pieces) + len(waits): 0} if carried else {},
        compiler_params=pltpu.CompilerParams(vmem_limit_bytes=12 * 2**20),
        cost_estimate=COST,
        name=name,
    )(base, *pieces, *waits, *carried)


def line_up(shares, width):
    def kernel(*refs):
        at = 0
        for ref in refs[:-1]:
            cols = ref.shape[1]
            refs[-1][:, at : at + cols] = ref[0:1, :]
            at += cols

    return pl.pallas_call(
        kernel,
        in_specs=[VMEM] * len(shares),
        out_specs=VMEM,
        out_shape=jax.ShapeDtypeStruct((1, width), F32),
        name="bias",
    )(*shares).reshape(width)


def back_kernel(index, jobs, base_ref, gp_ref, weight_ref, prop_ref, *rest):
    if jobs:
        out_ref, done_ref, whole_ref, sems = rest[-4:]
        copies = placing(base_ref, jobs, rest[: 2 * len(jobs)], whole_ref, sems)
    else:
        out_ref, done_ref = rest[-2:]
        copies = []
    part, cols = out_ref.shape
    j = pl.program_id(0)

    @pl.when(j == 0)
    def _():
        done_ref[...] = jnp.zeros_like(done_ref)
        for copy in copies:
            copy.start()

    cut = pl.ds(pl.multiple_of(j * cols, cols), cols)
    mixed = lax.dot_general(
        gp_ref[index * part : (index + 1) * part, :],
        weight_ref[cut, :],
        (((1,), (1,)), ((), ())),
        preferred_element_type=F32,
    ).astype(BF16)
    for t in range(part // TILE):
        rows = slice(t * TILE, (t + 1) * TILE)
        tile = index * (part // TILE) + t
        out_ref[rows, :] = jnp.dot(prop_ref[tile], mixed[rows], preferred_element_type=F32).astype(BF16)

    @pl.when(j == pl.num_programs(0) - 1)
    def _():
        for copy in copies:
            copy.wait()


def back(name, base, gp, weight, prop_t, waits, carried, index, count, jobs, pieces, out):
    rows, width = gp.shape
    part = rows // count
    cols = min(width, 1024)
    before = [] if carried is None else [carried]
    whole = [out] if jobs and out is not None else []
    at = 4 + len(pieces) + len(waits)
    aliases = {at: 0} if before else {}
    if whole:
        aliases[at + len(before)] = 2
    return pl.pallas_call(
        functools.partial(back_kernel, index, jobs),
        grid_spec=pltpu.PrefetchScalarGridSpec(
            num_scalar_prefetch=1,
            grid=(width // cols,),
            in_specs=[VMEM] * (3 + len(pieces)) + [ANY] * (len(waits) + len(before) + len(whole)),
            out_specs=[pl.BlockSpec((part, cols), lambda j, b: (index, j)), VMEM] + ([ANY] if jobs else []),
            scratch_shapes=[pltpu.SemaphoreType.DMA((8 * len(jobs),))] if jobs else [],
        ),
        out_shape=[jax.ShapeDtypeStruct((rows, width), BF16), DONE]
        + ([jax.ShapeDtypeStruct((width, width), F32)] if jobs else []),
        input_output_aliases=aliases,
        compiler_params=pltpu.CompilerParams(vmem_limit_bytes=20 * 2**20),
        cost_estimate=COST,
        name=name,
    )(base, gp, weight, prop_t, *pieces, *waits, *before, *whole)


def bit_length(n):
    return n.bit_length() - 1


def per_device(groups, locs, features, weight, bias, cotangent, neighbours, edge_mask, cluster_ids, row_mask):
    width = features.shape[1]
    devices = groups * locs
    top, low = bit_length(devices), bit_length(locs)
    y_bits, x_bits, z_bits = list(range(1, low)), list(range(low, top - 2)), [top - 2, top - 1]
    axes = ("grp", "loc")
    number = lax.axis_index("grp") * locs + lax.axis_index("loc")

    def swap(value, pair):
        flip = lambda i: i ^ (1 << pair[i & 1])
        return lax.ppermute(value, axes, [(i, flip(i)) for i in range(devices)])

    core, first, second, near_z = (0, 0), (x_bits[0], y_bits[0]), (y_bits[0], x_bits[0]), (z_bits[0],) * 2
    stages = {"x": first, "y": second, "z": near_z}
    halving = {kind: [stages[k] for k in kind] for _, kind in GROUPS}
    doubling = [(z_bits[1],) * 2] + [(b, b) for b in x_bits[1:] + y_bits[1:]]

    slots, line = [], {}
    for kind in sorted(halving):
        line[kind] = len(slots)
        for side in (1 - number % 2, number % 2):
            spot = side
            for pair in halving[kind]:
                spot = spot * 2 + jnp.where(side == 1, (number >> pair[1]) & 1, (number >> pair[0]) & 1)
            slots.append(spot)
    base = jnp.stack(slots).astype(jnp.int32)

    prop_t, mixed = propagate(features, neighbours, edge_mask, cluster_ids, row_mask, base)

    count = len(GROUPS)
    unit = width // sum(u for u, _ in GROUPS)
    starts, sizes, kinds = [], [], []
    for u, kind in GROUPS:
        starts.append(sum(sizes))
        sizes.append(u * unit)
        kinds.append(kind)
    fills = sum(e[0] == "f" for e in ORDER)

    terms = [None] * count
    got = [None] * count
    shares = [None] * count
    carried = []
    out = None
    grad_features = None
    token = prop_t
    end = width // 16

    flight = {}

    def halves(names):
        jobs, pieces = [], []
        for name in names:
            n, which = int(name[1]), int(name[2])
            jobs.append((line[kinds[n]] + 1 - which, starts[n]))
            pieces += terms[n] if which == 0 else got[n]
        return tuple(jobs), pieces

    for event in ORDER:
        event, *early = event.split("+")
        event, *riders = event.split("*")
        what, g = event[0], int(event[1])
        stage = int(event[2]) if len(event) > 2 else 0
        waits = [token] + [flight[name] for name in early]
        if what == "g":
            act, gp, theirs, mine = layer_group(
                event, base, line[kinds[g]], mixed, weight, bias, cotangent, waits, carried, starts[g], sizes[g]
            )
            carried = [act, gp]
            token = theirs
            terms[g] = [mine, swap(theirs, core)]
            flight[f"c{g}_"] = terms[g][1]
        elif what == "r" and stage < 3:
            n = (width // 2) >> (stage + 1)
            send, keep = join(
                event,
                terms[g],
                waits,
                ((n + 8, ((0, n), (1, n))),),
                ((n, ((0, 0), (1, 0))), (8, ((0, 2 * n), (1, 2 * n)))),
            )
            terms[g] = [keep, swap(send, halving[kinds[g]][stage])]
            flight[f"R{g}{stage}"] = terms[g][1]
            token = send
        elif what == "r":
            for pair in doubling:
                (total,) = join(event, terms[g], waits, ((end + 8, ((0, 0), (1, 0))),))
                terms[g] = [total, swap(total, pair)]
                token = total
                waits = [token]
            flight[f"R{g}{stage}"] = terms[g][1]
        elif what == "a":
            if stage == 0:
                total, shares[g] = join(
                    event, terms[g], waits, ((end, ((0, 0), (1, 0))),), ((8, ((0, end), (1, end))),)
                )
            else:
                n = terms[g][0].shape[0]
                (total,) = join(event, terms[g], waits, ((n, ((0, 0),)), (n, ((1, 0),))))
            terms[g] = [total, swap(total, halving[kinds[g]][2 - stage])]
            flight[f"A{g}{stage}"] = terms[g][1]
            if stage == 2:
                got[g] = [swap(total, core)]
                flight[f"C{g}0"] = got[g][0]
            token = total
        elif what == "c":
            late, _ = lax.optimization_barrier((terms[g][1], token))
            terms[g][1] = late
            got[g].append(swap(late, core))
            flight[f"C{g}1"] = got[g][1]
        elif what == "w":
            jobs, pieces = halves([event])
            out, token = place(event, base, jobs, pieces, waits, out, width)
        else:
            jobs, pieces = halves(riders)
            grad_features, token, *more = back(
                event, base, carried[1], weight, prop_t, waits, grad_features, g, fills, jobs, pieces, out
            )
            out = more[0] if more else out
    return carried[0], grad_features, out, line_up(shares, width)


def solution(mesh):
    rows = P(("grp", "loc"), None)
    flat = P(("grp", "loc"))
    in_specs = (rows, P(), P(), rows, rows, rows, flat, flat)
    out_specs = (rows, rows, P(), P())
    return jax.shard_map(
        functools.partial(per_device, mesh.shape["grp"], mesh.shape["loc"]),
        mesh=mesh,
        in_specs=in_specs,
        out_specs=out_specs,
        check_vma=False,
    )
```

```python
import functools

import jax
import jax.numpy as jnp
from jax import lax
from jax.experimental import pallas as pl
from jax.experimental.pallas import tpu as pltpu
from jax.sharding import PartitionSpec as P

TILE = 128
BF16 = jnp.bfloat16
F32 = jnp.float32

GROUPS = ((4, "xyz"), (4, "zxy"), (4, "xyz"), (4, "xyz"))
ORDER = (
    "g0", "g1", "r00", "g2", "r10", "r20", "r01", "g3", "f0", "r02+c3_", "r21", "r30", "r11", "r03", "r22",
    "f1", "r31", "a00", "r23", "r12", "r32", "a01", "r13", "a20", "a02", "r33", "a10+C00", "f2", "a21",
    "a30+A02+A10", "a11", "a22", "c0", "a31", "a12+C20", "w01", "a32+C10", "c2", "w20", "f3*w00*w21+C30", "c1",
    "w10", "c3", "w11", "w30", "w31",
)

COST = pl.CostEstimate(flops=25 * 10**9, bytes_accessed=2**20, transcendentals=0)
DONE = jax.ShapeDtypeStruct((8, 128), F32)
VMEM = pl.BlockSpec(memory_space=pltpu.VMEM)
ANY = pl.BlockSpec(memory_space=pl.ANY)


def tile_kernel(near_ref, live_ref, cluster_ref, present_ref, features_ref, base_ref, prop_ref, mixed_ref):
    tiles = cluster_ref.shape[0]
    step = pl.program_id(0)
    slot = lax.broadcasted_iota(jnp.int32, (TILE, TILE), 0)
    node = lax.broadcasted_iota(jnp.int32, (TILE, TILE), 1)
    slot_low = slot.astype(F32).astype(BF16)
    one, zero = jnp.ones((TILE, TILE), BF16), jnp.zeros((TILE, TILE), BF16)
    for t in range(tiles):
        part = slice(t * TILE, (t + 1) * TILE)
        near = jnp.where(live_ref[:, part] == 1, near_ref[:, part], -1).astype(F32).astype(BF16)
        hits = zero
        for k in range(near.shape[0]):
            hits = hits + jnp.where(near[k : k + 1, :] == slot_low, one, zero)
        key = jnp.where(present_ref[t] == 1, cluster_ref[t], -1).astype(F32)
        along = jnp.broadcast_to(key, (TILE, TILE))
        down = along.T
        allowed = (along == down) & (along >= 0.0) & (slot != node)
        adjacency = jnp.where(allowed, hits.astype(F32), 0.0)
        degree = jnp.sum(adjacency, axis=0, keepdims=True)
        self_loops = jnp.where((slot == node) & (along >= 0.0), 2.0, 0.0)
        prop_t = (adjacency + self_loops) / (degree + 1.0)
        at = step * tiles + t
        prop_ref[at] = prop_t.astype(BF16)
        prop = prop_t.T.astype(BF16)
        mixed = jnp.dot(prop, features_ref[part, :], preferred_element_type=F32)
        mixed_ref[pl.ds(pl.multiple_of(at * TILE, TILE), TILE), :] = mixed.astype(BF16)


def propagate(features, neighbours, edge_mask, cluster_ids, row_mask, base):
    rows, width = features.shape
    tiles = rows // TILE
    nbrs = neighbours.shape[1]
    each = 4
    block = each * TILE
    inputs = (
        neighbours.T,
        edge_mask.T,
        cluster_ids.reshape(tiles, 1, TILE),
        row_mask.reshape(tiles, 1, TILE),
        features,
    )
    return pl.pallas_call(
        tile_kernel,
        grid=(tiles // each,),
        in_specs=[
            pl.BlockSpec((nbrs, block), lambda t: (0, t)),
            pl.BlockSpec((nbrs, block), lambda t: (0, t)),
            pl.BlockSpec((each, 1, TILE), lambda t: (t, 0, 0)),
            pl.BlockSpec((each, 1, TILE), lambda t: (t, 0, 0)),
            pl.BlockSpec((block, width), lambda t: (t, 0)),
            ANY,
        ],
        out_specs=[VMEM, VMEM],
        out_shape=[
            jax.ShapeDtypeStruct((tiles, TILE, TILE), BF16),
            jax.ShapeDtypeStruct((rows, width), BF16),
        ],
        compiler_params=pltpu.CompilerParams(vmem_limit_bytes=12 * 2**20),
        cost_estimate=pl.CostEstimate(
            flops=2 * rows * width * width // 2, bytes_accessed=2 * rows * width, transcendentals=0
        ),
        name="propagate",
    )(*(pltpu.with_memory_space_constraint(v, pltpu.HBM) for v in inputs), base)


def layer_kernel(start, line, base_ref, mixed_ref, weight_ref, bias_ref, cot_ref, *rest):
    act_ref, cot_in, act_sem, cot_sem = rest[-4:]
    act_out, gp_ref, theirs_ref, mine_ref = rest[-8:-4]
    rows, cols = act_ref.shape
    block = min(rows, 512)
    half = mixed_ref.shape[1] // 4
    chunk = half // 4
    here = slice(start, start + cols)
    load = pltpu.make_async_copy(cot_ref.at[:, pl.ds(start, cols)], cot_in, cot_sem)
    load.start()
    total = jnp.zeros((1, cols), F32)
    for i in range(rows // block):
        part = slice(i * block, (i + 1) * block)
        pre = jnp.dot(mixed_ref[part, :], weight_ref[:, here], preferred_element_type=F32) + bias_ref[:, here]
        act_ref[part, :] = jnp.maximum(pre, 0.0).astype(BF16)
        if i == 0:
            load.wait()
        grad = jnp.where(pre > 0.0, cot_in[part, :].astype(F32), 0.0).astype(BF16)
        gp_ref[part, here] = grad
        total = total + jnp.sum(grad.astype(F32), axis=0, keepdims=True)
    store = pltpu.make_async_copy(act_ref, act_out.at[:, pl.ds(start, cols)], act_sem)
    store.start()

    def share_of(from_row):
        return lax.dot_general(
            mixed_ref[:, pl.ds(from_row, half)],
            gp_ref[:, here],
            (((0,), (0,)), ((), ())),
            preferred_element_type=F32,
        )

    total = jnp.broadcast_to(total, (8, cols))
    for side, out_ref in ((0, theirs_ref), (1, mine_ref)):
        for j in range(2):
            share = share_of(pl.multiple_of((base_ref[line + side] // 8) * 2 * half + j * half, half))
            for m in range(4):
                spot = ((j * 4 + m) ^ (base_ref[line + side] % 8)) * chunk
                out_ref[pl.ds(pl.multiple_of(spot, chunk), chunk), :] = share[m * chunk : (m + 1) * chunk]
        out_ref[2 * half :, :] = total
    store.wait()


def layer_group(name, base, line, mixed, weight, bias, cotangent, waits, carried, start, cols):
    rows, width = mixed.shape
    share = jax.ShapeDtypeStruct((width // 2 + 8, cols), F32)
    return pl.pallas_call(
        functools.partial(layer_kernel, start, line),
        grid_spec=pltpu.PrefetchScalarGridSpec(
            num_scalar_prefetch=1,
            grid=(1,),
            in_specs=[VMEM, VMEM, VMEM, ANY] + [ANY] * len(waits) + ([ANY, VMEM] if carried else []),
            out_specs=[ANY, VMEM, VMEM, VMEM],
            scratch_shapes=[
                pltpu.VMEM((rows, cols), BF16),
                pltpu.VMEM((rows, cols), BF16),
                pltpu.SemaphoreType.DMA,
                pltpu.SemaphoreType.DMA,
            ],
        ),
        out_shape=[
            jax.ShapeDtypeStruct((rows, width), BF16),
            jax.ShapeDtypeStruct((rows, width), BF16),
            share,
            share,
        ],
        input_output_aliases={5 + len(waits): 0, 6 + len(waits): 1} if carried else {},
        compiler_params=pltpu.CompilerParams(vmem_limit_bytes=10 * 2**20),
        cost_estimate=COST,
        name=name,
    )(
        base,
        mixed,
        weight,
        bias.reshape(1, width),
        pltpu.with_memory_space_constraint(cotangent, pltpu.HBM),
        *waits,
        *carried,
    )


def join_kernel(plan, *refs):
    outs = refs[len(refs) - len(plan) :]
    for out_ref, pieces in zip(outs, plan):
        at = 0
        for count, terms in pieces:
            value = refs[terms[0][0]][terms[0][1] : terms[0][1] + count, :]
            for index, row in terms[1:]:
                value = value + refs[index][row : row + count, :]
            out_ref[at : at + count, :] = value
            at += count


def join(name, arrays, waits, *plan):
    cols = arrays[0].shape[1]
    return pl.pallas_call(
        functools.partial(join_kernel, plan),
        in_specs=[VMEM] * len(arrays) + [ANY] * len(waits),
        out_specs=[VMEM] * len(plan),
        out_shape=[jax.ShapeDtypeStruct((sum(n for n, _ in pieces), cols), F32) for pieces in plan],
        compiler_params=pltpu.CompilerParams(vmem_limit_bytes=12 * 2**20),
        cost_estimate=COST,
        name=name,
    )(*arrays, *waits)


def placing(base_ref, jobs, refs, out_ref, sems):
    copies = []
    for n, (side, at) in enumerate(jobs):
        cols = refs[2 * n].shape[1]
        chunk = refs[2 * n].shape[0] // 4
        for r in range(8):
            spot = pl.multiple_of((base_ref[side] ^ r) * chunk, chunk)
            copies.append(
                pltpu.make_async_copy(
                    refs[2 * n + r // 4].at[pl.ds((r % 4) * chunk, chunk), :],
                    out_ref.at[pl.ds(spot, chunk), pl.ds(at, cols)],
                    sems.at[8 * n + r],
                )
            )
    return copies


def place_kernel(jobs, base_ref, *rest):
    out_ref, done_ref, sems = rest[-3:]
    copies = placing(base_ref, jobs, rest[: 2 * len(jobs)], out_ref, sems)
    for copy in copies:
        copy.start()
    done_ref[...] = jnp.zeros_like(done_ref)
    for copy in copies:
        copy.wait()


def place(name, base, jobs, pieces, waits, out, width):
    carried = [] if out is None else [out]
    return pl.pallas_call(
        functools.partial(place_kernel, jobs),
        grid_spec=pltpu.PrefetchScalarGridSpec(
            num_scalar_prefetch=1,
            grid=(1,),
            in_specs=[VMEM] * len(pieces) + [ANY] * (len(waits) + len(carried)),
            out_specs=[ANY, VMEM],
            scratch_shapes=[pltpu.SemaphoreType.DMA((8 * len(jobs),))],
        ),
        out_shape=[jax.ShapeDtypeStruct((width, width), F32), DONE],
        input_output_aliases={1 + len(pieces) + len(waits): 0} if carried else {},
        compiler_params=pltpu.CompilerParams(vmem_limit_bytes=12 * 2**20),
        cost_estimate=COST,
        name=name,
    )(base, *pieces, *waits, *carried)


def line_up(shares, width):
    def kernel(*refs):
        at = 0
        for ref in refs[:-1]:
            cols = ref.shape[1]
            refs[-1][:, at : at + cols] = ref[0:1, :]
            at += cols

    return pl.pallas_call(
        kernel,
        in_specs=[VMEM] * len(shares),
        out_specs=VMEM,
        out_shape=jax.ShapeDtypeStruct((1, width), F32),
        name="bias",
    )(*shares).reshape(width)


def back_kernel(index, jobs, base_ref, gp_ref, weight_ref, prop_ref, *rest):
    if jobs:
        out_ref, done_ref, whole_ref, sems = rest[-4:]
        copies = placing(base_ref, jobs, rest[: 2 * len(jobs)], whole_ref, sems)
    else:
        out_ref, done_ref = rest[-2:]
        copies = []
    part, cols = out_ref.shape
    j = pl.program_id(0)

    @pl.when(j == 0)
    def _():
        done_ref[...] = jnp.zeros_like(done_ref)
        for copy in copies:
            copy.start()

    cut = pl.ds(pl.multiple_of(j * cols, cols), cols)
    mixed = lax.dot_general(
        gp_ref[index * part : (index + 1) * part, :],
        weight_ref[cut, :],
        (((1,), (1,)), ((), ())),
        preferred_element_type=F32,
    ).astype(BF16)
    for t in range(part // TILE):
        rows = slice(t * TILE, (t + 1) * TILE)
        tile = index * (part // TILE) + t
        out_ref[rows, :] = jnp.dot(prop_ref[tile], mixed[rows], preferred_element_type=F32).astype(BF16)

    @pl.when(j == pl.num_programs(0) - 1)
    def _():
        for copy in copies:
            copy.wait()


def back(name, base, gp, weight, prop_t, waits, carried, index, count, jobs, pieces, out):
    rows, width = gp.shape
    part = rows // count
    cols = min(width, 1024)
    before = [] if carried is None else [carried]
    whole = [out] if jobs and out is not None else []
    at = 4 + len(pieces) + len(waits)
    aliases = {at: 0} if before else {}
    if whole:
        aliases[at + len(before)] = 2
    return pl.pallas_call(
        functools.partial(back_kernel, index, jobs),
        grid_spec=pltpu.PrefetchScalarGridSpec(
            num_scalar_prefetch=1,
            grid=(width // cols,),
            in_specs=[VMEM] * (3 + len(pieces)) + [ANY] * (len(waits) + len(before) + len(whole)),
            out_specs=[pl.BlockSpec((part, cols), lambda j, b: (index, j)), VMEM] + ([ANY] if jobs else []),
            scratch_shapes=[pltpu.SemaphoreType.DMA((8 * len(jobs),))] if jobs else [],
        ),
        out_shape=[jax.ShapeDtypeStruct((rows, width), BF16), DONE]
        + ([jax.ShapeDtypeStruct((width, width), F32)] if jobs else []),
        input_output_aliases=aliases,
        compiler_params=pltpu.CompilerParams(vmem_limit_bytes=20 * 2**20),
        cost_estimate=COST,
        name=name,
    )(base, gp, weight, prop_t, *pieces, *waits, *before, *whole)


def bit_length(n):
    return n.bit_length() - 1


def per_device(groups, locs, features, weight, bias, cotangent, neighbours, edge_mask, cluster_ids, row_mask):
    width = features.shape[1]
    devices = groups * locs
    top, low = bit_length(devices), bit_length(locs)
    y_bits, x_bits, z_bits = list(range(1, low)), list(range(low, top - 2)), [top - 2, top - 1]
    axes = ("grp", "loc")
    number = lax.axis_index("grp") * locs + lax.axis_index("loc")

    def swap(value, pair):
        return lax.ppermute(value, axes, [(i, i ^ pair[i & 1]) for i in range(devices)])

    x, y, z, far_z = 1 << x_bits[0], 1 << y_bits[0], 1 << z_bits[0], 3 << z_bits[0]
    core, first, second, near_z = (1, 1), (x, y), (y, x), (z, z)
    stages = {"x": first, "y": second, "z": near_z}
    halving = {kind: [stages[k] for k in kind] for _, kind in GROUPS}
    doubling = [(far_z, far_z)] + [(1 << b, 1 << b) for b in x_bits[1:] + y_bits[1:]]

    def side_of(mask):
        bit = (number & mask) != 0
        return (bit ^ ((number & (mask << 1)) != 0) if mask == z else bit).astype(jnp.int32)


    slots, line = [], {}
    for kind in sorted(halving):
        line[kind] = len(slots)
        for side in (1 - number % 2, number % 2):
            spot = side
            for pair in halving[kind]:
                spot = spot * 2 + jnp.where(side == 1, side_of(pair[1]), side_of(pair[0]))
            slots.append(spot)
    base = jnp.stack(slots).astype(jnp.int32)

    prop_t, mixed = propagate(features, neighbours, edge_mask, cluster_ids, row_mask, base)

    count = len(GROUPS)
    unit = width // sum(u for u, _ in GROUPS)
    starts, sizes, kinds = [], [], []
    for u, kind in GROUPS:
        starts.append(sum(sizes))
        sizes.append(u * unit)
        kinds.append(kind)
    fills = sum(e[0] == "f" for e in ORDER)

    terms = [None] * count
    got = [None] * count
    shares = [None] * count
    carried = []
    out = None
    grad_features = None
    token = prop_t
    end = width // 16

    flight = {}

    def halves(names):
        jobs, pieces = [], []
        for name in names:
            n, which = int(name[1]), int(name[2])
            jobs.append((line[kinds[n]] + 1 - which, starts[n]))
            pieces += terms[n] if which == 0 else got[n]
        return tuple(jobs), pieces

    for event in ORDER:
        event, *early = event.split("+")
        event, *riders = event.split("*")
        what, g = event[0], int(event[1])
        stage = int(event[2]) if len(event) > 2 else 0
        waits = [token] + [flight[name] for name in early]
        if what == "g":
            act, gp, theirs, mine = layer_group(
                event, base, line[kinds[g]], mixed, weight, bias, cotangent, waits, carried, starts[g], sizes[g]
            )
            carried = [act, gp]
            token = theirs
            terms[g] = [mine, swap(theirs, core)]
            flight[f"c{g}_"] = terms[g][1]
        elif what == "r" and stage < 3:
            n = (width // 2) >> (stage + 1)
            send, keep = join(
                event,
                terms[g],
                waits,
                ((n + 8, ((0, n), (1, n))),),
                ((n, ((0, 0), (1, 0))), (8, ((0, 2 * n), (1, 2 * n)))),
            )
            terms[g] = [keep, swap(send, halving[kinds[g]][stage])]
            flight[f"R{g}{stage}"] = terms[g][1]
            token = send
        elif what == "r":
            for pair in doubling:
                (total,) = join(event, terms[g], waits, ((end + 8, ((0, 0), (1, 0))),))
                terms[g] = [total, swap(total, pair)]
                token = total
                waits = [token]
            flight[f"R{g}{stage}"] = terms[g][1]
        elif what == "a":
            if stage == 0:
                total, shares[g] = join(
                    event, terms[g], waits, ((end, ((0, 0), (1, 0))),), ((8, ((0, end), (1, end))),)
                )
            else:
                n = terms[g][0].shape[0]
                (total,) = join(event, terms[g], waits, ((n, ((0, 0),)), (n, ((1, 0),))))
            terms[g] = [total, swap(total, halving[kinds[g]][2 - stage])]
            flight[f"A{g}{stage}"] = terms[g][1]
            if stage == 2:
                got[g] = [swap(total, core)]
                flight[f"C{g}0"] = got[g][0]
            token = total
        elif what == "c":
            late, _ = lax.optimization_barrier((terms[g][1], token))
            terms[g][1] = late
            got[g].append(swap(late, core))
            flight[f"C{g}1"] = got[g][1]
        elif what == "w":
            jobs, pieces = halves([event])
            out, token = place(event, base, jobs, pieces, waits, out, width)
        else:
            jobs, pieces = halves(riders)
            grad_features, token, *more = back(
                event, base, carried[1], weight, prop_t, waits, grad_features, g, fills, jobs, pieces, out
            )
            out = more[0] if more else out
    return carried[0], grad_features, out, line_up(shares, width)


def solution(mesh):
    rows = P(("grp", "loc"), None)
    flat = P(("grp", "loc"))
    in_specs = (rows, P(), P(), rows, rows, rows, flat, flat)
    out_specs = (rows, rows, P(), P())
    return jax.shard_map(
        functools.partial(per_device, mesh.shape["grp"], mesh.shape["loc"]),
        mesh=mesh,
        in_specs=in_specs,
        out_specs=out_specs,
        check_vma=False,
    )
```

```python
import functools

import jax
import jax.numpy as jnp
from jax import lax
from jax.experimental import pallas as pl
from jax.experimental.pallas import tpu as pltpu
from jax.sharding import PartitionSpec as P

TILE = 128
BF16 = jnp.bfloat16
F32 = jnp.float32

GROUPS = ((4, "xyz"), (4, "zxy"), (4, "xyz"), (4, "xyz"))
ORDER = (
    "g0", "g1", "r00", "g2", "r10", "r20", "r01", "g3", "f0", "r02+c3_", "r21", "r30", "r11", "r03", "r22",
    "f1", "r31", "a00", "r23", "r12", "r32", "a01", "r13", "a20", "a02", "f2", "r33+C00", "a10", "a21",
    "a30+A02+A10", "a11", "a22", "c0", "a31", "a12+C01+C20", "w01", "a32+C10", "w00", "c2", "w20",
    "f3*w21+C30", "c1", "w10", "c3", "w11", "w30", "w31",
)

COST = pl.CostEstimate(flops=25 * 10**9, bytes_accessed=2**20, transcendentals=0)
DONE = jax.ShapeDtypeStruct((8, 128), F32)
VMEM = pl.BlockSpec(memory_space=pltpu.VMEM)
ANY = pl.BlockSpec(memory_space=pl.ANY)


def tile_kernel(near_ref, live_ref, cluster_ref, present_ref, features_ref, base_ref, prop_ref, mixed_ref):
    tiles = cluster_ref.shape[0]
    step = pl.program_id(0)
    slot = lax.broadcasted_iota(jnp.int32, (TILE, TILE), 0)
    node = lax.broadcasted_iota(jnp.int32, (TILE, TILE), 1)
    slot_low = slot.astype(F32).astype(BF16)
    one, zero = jnp.ones((TILE, TILE), BF16), jnp.zeros((TILE, TILE), BF16)
    for t in range(tiles):
        part = slice(t * TILE, (t + 1) * TILE)
        near = jnp.where(live_ref[:, part] == 1, near_ref[:, part], -1).astype(F32).astype(BF16)
        hits = zero
        for k in range(near.shape[0]):
            hits = hits + jnp.where(near[k : k + 1, :] == slot_low, one, zero)
        key = jnp.where(present_ref[t] == 1, cluster_ref[t], -1).astype(F32)
        along = jnp.broadcast_to(key, (TILE, TILE))
        down = along.T
        allowed = (along == down) & (along >= 0.0) & (slot != node)
        adjacency = jnp.where(allowed, hits.astype(F32), 0.0)
        degree = jnp.sum(adjacency, axis=0, keepdims=True)
        self_loops = jnp.where((slot == node) & (along >= 0.0), 2.0, 0.0)
        prop_t = (adjacency + self_loops) / (degree + 1.0)
        at = step * tiles + t
        prop_ref[at] = prop_t.astype(BF16)
        prop = prop_t.T.astype(BF16)
        mixed = jnp.dot(prop, features_ref[part, :], preferred_element_type=F32)
        mixed_ref[pl.ds(pl.multiple_of(at * TILE, TILE), TILE), :] = mixed.astype(BF16)


def propagate(features, neighbours, edge_mask, cluster_ids, row_mask, base):
    rows, width = features.shape
    tiles = rows // TILE
    nbrs = neighbours.shape[1]
    each = 4
    block = each * TILE
    inputs = (
        neighbours.T,
        edge_mask.T,
        cluster_ids.reshape(tiles, 1, TILE),
        row_mask.reshape(tiles, 1, TILE),
        features,
    )
    return pl.pallas_call(
        tile_kernel,
        grid=(tiles // each,),
        in_specs=[
            pl.BlockSpec((nbrs, block), lambda t: (0, t)),
            pl.BlockSpec((nbrs, block), lambda t: (0, t)),
            pl.BlockSpec((each, 1, TILE), lambda t: (t, 0, 0)),
            pl.BlockSpec((each, 1, TILE), lambda t: (t, 0, 0)),
            pl.BlockSpec((block, width), lambda t: (t, 0)),
            ANY,
        ],
        out_specs=[VMEM, VMEM],
        out_shape=[
            jax.ShapeDtypeStruct((tiles, TILE, TILE), BF16),
            jax.ShapeDtypeStruct((rows, width), BF16),
        ],
        compiler_params=pltpu.CompilerParams(vmem_limit_bytes=12 * 2**20),
        cost_estimate=pl.CostEstimate(
            flops=2 * rows * width * width // 2, bytes_accessed=2 * rows * width, transcendentals=0
        ),
        name="propagate",
    )(*(pltpu.with_memory_space_constraint(v, pltpu.HBM) for v in inputs), base)


def emit_half(slot, here, base_ref, mixed_ref, gp_ref, total, out_ref):
    half = mixed_ref.shape[1] // 4
    chunk = half // 4
    for j in range(2):
        from_row = pl.multiple_of((base_ref[slot] // 8) * 2 * half + j * half, half)
        share = lax.dot_general(
            mixed_ref[:, pl.ds(from_row, half)],
            gp_ref[:, here],
            (((0,), (0,)), ((), ())),
            preferred_element_type=F32,
        )
        for m in range(4):
            spot = ((j * 4 + m) ^ (base_ref[slot] % 8)) * chunk
            out_ref[pl.ds(pl.multiple_of(spot, chunk), chunk), :] = share[m * chunk : (m + 1) * chunk]
    out_ref[2 * half :, :] = total


def layer_kernel(start, line, halves, base_ref, mixed_ref, weight_ref, bias_ref, cot_ref, *rest):
    act_ref, cot_in, act_sem, cot_sem = rest[-4:]
    act_out, gp_ref, *outs = rest[-6 - halves : -4]
    rows, cols = act_ref.shape
    block = min(rows, 512)
    here = slice(start, start + cols)
    load = pltpu.make_async_copy(cot_ref.at[:, pl.ds(start, cols)], cot_in, cot_sem)
    load.start()
    total = jnp.zeros((1, cols), F32)
    for i in range(rows // block):
        part = slice(i * block, (i + 1) * block)
        pre = jnp.dot(mixed_ref[part, :], weight_ref[:, here], preferred_element_type=F32) + bias_ref[:, here]
        act_ref[part, :] = jnp.maximum(pre, 0.0).astype(BF16)
        if i == 0:
            load.wait()
        grad = jnp.where(pre > 0.0, cot_in[part, :].astype(F32), 0.0).astype(BF16)
        gp_ref[part, here] = grad
        total = total + jnp.sum(grad.astype(F32), axis=0, keepdims=True)
    store = pltpu.make_async_copy(act_ref, act_out.at[:, pl.ds(start, cols)], act_sem)
    store.start()

    total = jnp.broadcast_to(total, (8, cols))
    for side, out_ref in enumerate(outs):
        emit_half(line + side, here, base_ref, mixed_ref, gp_ref, total, out_ref)
    store.wait()


def other_half_kernel(slot, start, base_ref, mixed_ref, gp_ref, theirs_ref, *rest):
    out_ref = rest[-1]
    here = slice(start, start + out_ref.shape[1])
    emit_half(slot, here, base_ref, mixed_ref, gp_ref, theirs_ref[out_ref.shape[0] - 8 :, :], out_ref)


def other_half(name, base, slot, mixed, gp, theirs, waits, start):
    return pl.pallas_call(
        functools.partial(other_half_kernel, slot, start),
        grid_spec=pltpu.PrefetchScalarGridSpec(
            num_scalar_prefetch=1,
            grid=(1,),
            in_specs=[VMEM] * 3 + [ANY] * len(waits),
            out_specs=VMEM,
        ),
        out_shape=jax.ShapeDtypeStruct(theirs.shape, F32),
        compiler_params=pltpu.CompilerParams(vmem_limit_bytes=10 * 2**20),
        cost_estimate=COST,
        name=name,
    )(base, mixed, gp, theirs, *waits)


def layer_group(name, base, line, halves, mixed, weight, bias, cotangent, waits, carried, start, cols):
    rows, width = mixed.shape
    share = jax.ShapeDtypeStruct((width // 2 + 8, cols), F32)
    return pl.pallas_call(
        functools.partial(layer_kernel, start, line, halves),
        grid_spec=pltpu.PrefetchScalarGridSpec(
            num_scalar_prefetch=1,
            grid=(1,),
            in_specs=[VMEM, VMEM, VMEM, ANY] + [ANY] * len(waits) + ([ANY, VMEM] if carried else []),
            out_specs=[ANY, VMEM] + [VMEM] * halves,
            scratch_shapes=[
                pltpu.VMEM((rows, cols), BF16),
                pltpu.VMEM((rows, cols), BF16),
                pltpu.SemaphoreType.DMA,
                pltpu.SemaphoreType.DMA,
            ],
        ),
        out_shape=[
            jax.ShapeDtypeStruct((rows, width), BF16),
            jax.ShapeDtypeStruct((rows, width), BF16),
        ]
        + [share] * halves,
        input_output_aliases={5 + len(waits): 0, 6 + len(waits): 1} if carried else {},
        compiler_params=pltpu.CompilerParams(vmem_limit_bytes=10 * 2**20),
        cost_estimate=COST,
        name=name,
    )(
        base,
        mixed,
        weight,
        bias.reshape(1, width),
        pltpu.with_memory_space_constraint(cotangent, pltpu.HBM),
        *waits,
        *carried,
    )


def join_kernel(plan, *refs):
    outs = refs[len(refs) - len(plan) :]
    for out_ref, pieces in zip(outs, plan):
        at = 0
        for count, terms in pieces:
            value = refs[terms[0][0]][terms[0][1] : terms[0][1] + count, :]
            for index, row in terms[1:]:
                value = value + refs[index][row : row + count, :]
            out_ref[at : at + count, :] = value
            at += count


def join(name, arrays, waits, *plan):
    cols = arrays[0].shape[1]
    return pl.pallas_call(
        functools.partial(join_kernel, plan),
        in_specs=[VMEM] * len(arrays) + [ANY] * len(waits),
        out_specs=[VMEM] * len(plan),
        out_shape=[jax.ShapeDtypeStruct((sum(n for n, _ in pieces), cols), F32) for pieces in plan],
        compiler_params=pltpu.CompilerParams(vmem_limit_bytes=12 * 2**20),
        cost_estimate=COST,
        name=name,
    )(*arrays, *waits)


def placing(base_ref, jobs, refs, out_ref, sems):
    copies = []
    for n, (side, at) in enumerate(jobs):
        cols = refs[2 * n].shape[1]
        chunk = refs[2 * n].shape[0] // 4
        for r in range(8):
            spot = pl.multiple_of((base_ref[side] ^ r) * chunk, chunk)
            copies.append(
                pltpu.make_async_copy(
                    refs[2 * n + r // 4].at[pl.ds((r % 4) * chunk, chunk), :],
                    out_ref.at[pl.ds(spot, chunk), pl.ds(at, cols)],
                    sems.at[8 * n + r],
                )
            )
    return copies


def place_kernel(jobs, base_ref, *rest):
    out_ref, done_ref, sems = rest[-3:]
    copies = placing(base_ref, jobs, rest[: 2 * len(jobs)], out_ref, sems)
    for copy in copies:
        copy.start()
    done_ref[...] = jnp.zeros_like(done_ref)
    for copy in copies:
        copy.wait()


def place(name, base, jobs, pieces, waits, out, width):
    carried = [] if out is None else [out]
    return pl.pallas_call(
        functools.partial(place_kernel, jobs),
        grid_spec=pltpu.PrefetchScalarGridSpec(
            num_scalar_prefetch=1,
            grid=(1,),
            in_specs=[VMEM] * len(pieces) + [ANY] * (len(waits) + len(carried)),
            out_specs=[ANY, VMEM],
            scratch_shapes=[pltpu.SemaphoreType.DMA((8 * len(jobs),))],
        ),
        out_shape=[jax.ShapeDtypeStruct((width, width), F32), DONE],
        input_output_aliases={1 + len(pieces) + len(waits): 0} if carried else {},
        compiler_params=pltpu.CompilerParams(vmem_limit_bytes=12 * 2**20),
        cost_estimate=COST,
        name=name,
    )(base, *pieces, *waits, *carried)


def line_up(shares, width):
    def kernel(*refs):
        at = 0
        for ref in refs[:-1]:
            cols = ref.shape[1]
            refs[-1][:, at : at + cols] = ref[0:1, :]
            at += cols

    return pl.pallas_call(
        kernel,
        in_specs=[VMEM] * len(shares),
        out_specs=VMEM,
        out_shape=jax.ShapeDtypeStruct((1, width), F32),
        name="bias",
    )(*shares).reshape(width)


def back_kernel(index, jobs, base_ref, gp_ref, weight_ref, prop_ref, *rest):
    if jobs:
        out_ref, done_ref, whole_ref, sems = rest[-4:]
        copies = placing(base_ref, jobs, rest[: 2 * len(jobs)], whole_ref, sems)
    else:
        out_ref, done_ref = rest[-2:]
        copies = []
    part, cols = out_ref.shape
    j = pl.program_id(0)

    @pl.when(j == 0)
    def _():
        done_ref[...] = jnp.zeros_like(done_ref)
        for copy in copies:
            copy.start()

    cut = pl.ds(pl.multiple_of(j * cols, cols), cols)
    mixed = lax.dot_general(
        gp_ref[index * part : (index + 1) * part, :],
        weight_ref[cut, :],
        (((1,), (1,)), ((), ())),
        preferred_element_type=F32,
    ).astype(BF16)
    for t in range(part // TILE):
        rows = slice(t * TILE, (t + 1) * TILE)
        tile = index * (part // TILE) + t
        out_ref[rows, :] = jnp.dot(prop_ref[tile], mixed[rows], preferred_element_type=F32).astype(BF16)

    @pl.when(j == pl.num_programs(0) - 1)
    def _():
        for copy in copies:
            copy.wait()


def back(name, base, gp, weight, prop_t, waits, carried, index, count, jobs, pieces, out):
    rows, width = gp.shape
    part = rows // count
    cols = min(width, 1024)
    before = [] if carried is None else [carried]
    whole = [out] if jobs and out is not None else []
    at = 4 + len(pieces) + len(waits)
    aliases = {at: 0} if before else {}
    if whole:
        aliases[at + len(before)] = 2
    return pl.pallas_call(
        functools.partial(back_kernel, index, jobs),
        grid_spec=pltpu.PrefetchScalarGridSpec(
            num_scalar_prefetch=1,
            grid=(width // cols,),
            in_specs=[VMEM] * (3 + len(pieces)) + [ANY] * (len(waits) + len(before) + len(whole)),
            out_specs=[pl.BlockSpec((part, cols), lambda j, b: (index, j)), VMEM] + ([ANY] if jobs else []),
            scratch_shapes=[pltpu.SemaphoreType.DMA((8 * len(jobs),))] if jobs else [],
        ),
        out_shape=[jax.ShapeDtypeStruct((rows, width), BF16), DONE]
        + ([jax.ShapeDtypeStruct((width, width), F32)] if jobs else []),
        input_output_aliases=aliases,
        compiler_params=pltpu.CompilerParams(vmem_limit_bytes=20 * 2**20),
        cost_estimate=COST,
        name=name,
    )(base, gp, weight, prop_t, *pieces, *waits, *before, *whole)


def bit_length(n):
    return n.bit_length() - 1


def per_device(groups, locs, features, weight, bias, cotangent, neighbours, edge_mask, cluster_ids, row_mask):
    width = features.shape[1]
    devices = groups * locs
    top, low = bit_length(devices), bit_length(locs)
    y_bits, x_bits, z_bits = list(range(1, low)), list(range(low, top - 2)), [top - 2, top - 1]
    axes = ("grp", "loc")
    number = lax.axis_index("grp") * locs + lax.axis_index("loc")

    def swap(value, pair):
        return lax.ppermute(value, axes, [(i, i ^ pair[i & 1]) for i in range(devices)])

    x, y, z, far_z = 1 << x_bits[0], 1 << y_bits[0], 1 << z_bits[0], 3 << z_bits[0]
    core, first, second, near_z = (1, 1), (x, y), (y, x), (z, z)
    stages = {"x": first, "y": second, "z": near_z}
    halving = {kind: [stages[k] for k in kind] for _, kind in GROUPS}
    doubling = [(far_z, far_z)] + [(1 << b, 1 << b) for b in x_bits[1:] + y_bits[1:]]

    def side_of(mask):
        bit = (number & mask) != 0
        return (bit ^ ((number & (mask << 1)) != 0) if mask == z else bit).astype(jnp.int32)


    slots, line = [], {}
    for kind in sorted(halving):
        line[kind] = len(slots)
        for side in (1 - number % 2, number % 2):
            spot = side
            for pair in halving[kind]:
                spot = spot * 2 + jnp.where(side == 1, side_of(pair[1]), side_of(pair[0]))
            slots.append(spot)
    base = jnp.stack(slots).astype(jnp.int32)

    prop_t, mixed = propagate(features, neighbours, edge_mask, cluster_ids, row_mask, base)

    count = len(GROUPS)
    unit = width // sum(u for u, _ in GROUPS)
    starts, sizes, kinds = [], [], []
    for u, kind in GROUPS:
        starts.append(sum(sizes))
        sizes.append(u * unit)
        kinds.append(kind)
    fills = sum(e[0] == "f" for e in ORDER)

    terms = [None] * count
    got = [None] * count
    shares = [None] * count
    carried = []
    out = None
    grad_features = None
    token = prop_t
    end = width // 16

    flight, sent = {}, {}

    def halves(names):
        jobs, pieces = [], []
        for name in names:
            n, which = int(name[1]), int(name[2])
            jobs.append((line[kinds[n]] + 1 - which, starts[n]))
            pieces += terms[n] if which == 0 else got[n]
        return tuple(jobs), pieces

    for event in ORDER:
        event, *early = event.split("+")
        event, *riders = event.split("*")
        what, g = event[0], int(event[1])
        stage = int(event[2]) if len(event) > 2 else 0
        waits = [token] + [flight[name] for name in early]
        if what == "g":
            act, gp, theirs, *mine = layer_group(
                event,
                base,
                line[kinds[g]],
                1 if f"m{g}" in ORDER else 2,
                mixed,
                weight,
                bias,
                cotangent,
                waits,
                carried,
                starts[g],
                sizes[g],
            )
            carried = [act, gp]
            sent[g] = theirs
            terms[g] = mine + [swap(theirs, core)]
            flight[f"c{g}_"] = terms[g][-1]
            token = theirs
        elif what == "m":
            token = other_half(event, base, line[kinds[g]] + 1, mixed, carried[1], sent[g], waits, starts[g])
            terms[g] = [token] + terms[g]
        elif what == "r" and stage < 3:
            n = (width // 2) >> (stage + 1)
            send, keep = join(
                event,
                terms[g],
                waits,
                ((n + 8, ((0, n), (1, n))),),
                ((n, ((0, 0), (1, 0))), (8, ((0, 2 * n), (1, 2 * n)))),
            )
            terms[g] = [keep, swap(send, halving[kinds[g]][stage])]
            flight[f"R{g}{stage}"] = terms[g][1]
            token = send
        elif what == "r":
            for pair in doubling:
                (total,) = join(event, terms[g], waits, ((end + 8, ((0, 0), (1, 0))),))
                terms[g] = [total, swap(total, pair)]
                token = total
                waits = [token]
            flight[f"R{g}{stage}"] = terms[g][1]
        elif what == "a":
            if stage == 0:
                total, shares[g] = join(
                    event, terms[g], waits, ((end, ((0, 0), (1, 0))),), ((8, ((0, end), (1, end))),)
                )
            else:
                n = terms[g][0].shape[0]
                (total,) = join(event, terms[g], waits, ((n, ((0, 0),)), (n, ((1, 0),))))
            terms[g] = [total, swap(total, halving[kinds[g]][2 - stage])]
            flight[f"A{g}{stage}"] = terms[g][1]
            if stage == 2:
                got[g] = [swap(total, core)]
                flight[f"C{g}0"] = got[g][0]
            token = total
        elif what == "c":
            late, _ = lax.optimization_barrier((terms[g][1], token))
            terms[g][1] = late
            got[g].append(swap(late, core))
            flight[f"C{g}1"] = got[g][1]
        elif what == "w":
            jobs, pieces = halves([event])
            out, token = place(event, base, jobs, pieces, waits, out, width)
        else:
            jobs, pieces = halves(riders)
            grad_features, token, *more = back(
                event, base, carried[1], weight, prop_t, waits, grad_features, g, fills, jobs, pieces, out
            )
            out = more[0] if more else out
    return carried[0], grad_features, out, line_up(shares, width)


def solution(mesh):
    rows = P(("grp", "loc"), None)
    flat = P(("grp", "loc"))
    in_specs = (rows, P(), P(), rows, rows, rows, flat, flat)
    out_specs = (rows, rows, P(), P())
    return jax.shard_map(
        functools.partial(per_device, mesh.shape["grp"], mesh.shape["loc"]),
        mesh=mesh,
        in_specs=in_specs,
        out_specs=out_specs,
        check_vma=False,
    )
```
